32 devices in a mesh: rows: 8 (over z, y), grp: 4 (over x, core).
Axes of the slice: x: 2, y: 2, z: 4, core: 2. Of those that a mesh axis runs over, the one named last changes fastest.
Arguments:
- embeddings: float32 [4096, 768], P(('rows', 'grp')), may hold values from -100 to 100
- assignments: int32 [4096], P(('rows', 'grp')), may hold values from 0 to 16383, as said below
Outputs:
- whitened: float32 [4096, 768], P(('rows', 'grp'))
- centroid_means: float32 [16384, 768], P(('rows', 'grp'))
The draws below stay inside these ranges and needn't reach their ends.
Inputs may be any that keep to these rules, and one draw needn't show every extreme that they name: `assignments`: owner o holds the 2048 centroids o * 2048 to (o + 1) * 2048 - 1. The 128 rows of one device name centroids of at most 32 rows for any one owner, and exactly 32 for some owner. Some centroids are named by no row.
All inputs are finite; a program needn't handle non-finite values.
Results may differ from the reference program's by a relative error of at most 0.00007.
Values sent between devices are 32-bit elements; how exact they have to be, the bound alone decides.
A program may use at most 64 MiB of HBM per device.

```python
import math
import jax
import jax.numpy as jnp
from jax import lax

D = 768
CENTROIDS = 16384
R_DEV = 128
CAP = 32
TOTAL_ROWS = 4096
N_ROWS = 8


def draw_embeddings(key, part):
    first, second = jax.random.split(jax.random.fold_in(key, 11), 2)
    blocks = TOTAL_ROWS // R_DEV
    block_index = jnp.arange(TOTAL_ROWS, dtype=jnp.int32) // R_DEV
    device_scale = 3.0 ** (0.5 * block_index.astype(jnp.float32) / max(blocks - 1, 1))
    base = jnp.clip(jax.random.normal(first, (TOTAL_ROWS, D), jnp.float32), -5.0, 5.0)
    row_scale = jnp.exp(jax.random.uniform(second, (TOTAL_ROWS,), jnp.float32, 0.0, math.log(10.0)))
    values = base * row_scale[:, None]
    return values * device_scale[:, None]


def draw_assignments(key, part):
    per_owner = CENTROIDS // N_ROWS
    blocks = TOTAL_ROWS // R_DEV
    offsets = jax.random.randint(jax.random.fold_in(key, 7), (N_ROWS,), 0, per_owner)
    block_keys = jax.random.split(jax.random.fold_in(key, 5), blocks)

    def one_block(block_key):
        kfirst, ksecond, kthird, kfourth = jax.random.split(block_key, 4)
        chosen = jax.random.randint(kfirst, (), 0, N_ROWS)
        others = jnp.tile(jnp.arange(1, N_ROWS, dtype=jnp.int32), CAP)
        others = jax.random.permutation(ksecond, others)[:R_DEV - CAP]
        owners = jnp.concatenate([jnp.zeros((CAP,), jnp.int32), others])
        owners = (owners + chosen) % N_ROWS
        owners = jax.random.permutation(kthird, owners)
        tries = jax.random.randint(kfourth, (3, R_DEV), 0, per_owner)
        local = (jnp.min(tries, axis=0) + offsets[owners]) % per_owner
        return owners * per_owner + local
    return jax.vmap(one_block)(block_keys).reshape(TOTAL_ROWS).astype(jnp.int32)


def setup_inputs(seed: int = 0) -> dict:
    streams_of = jax.random.split(jax.random.key(seed), 3)
    return {
        "embeddings": draw_embeddings(jax.random.fold_in(streams_of[2], 71), 0),
        "assignments": draw_assignments(jax.random.fold_in(streams_of[2], 71), 0),
    }


def reference(embeddings, assignments):
    total = embeddings.shape[0]
    width = embeddings.shape[1]
    gram = jnp.dot(embeddings.T.astype(jnp.float32), embeddings.astype(jnp.float32), precision=lax.Precision.HIGHEST, preferred_element_type=jnp.float32)
    gram = gram / total + 1e-05 * jnp.eye(width, dtype=jnp.float32)
    factor = jnp.linalg.cholesky(gram)
    whitened = lax.linalg.triangular_solve(factor, embeddings, left_side=False, lower=True, transpose_a=True)
    list_sums = jax.ops.segment_sum(whitened, assignments, num_segments=CENTROIDS)
    ones = jnp.ones(assignments.shape, dtype=jnp.float32)
    list_counts = jax.ops.segment_sum(ones, assignments, num_segments=CENTROIDS)
    centroid_means = list_sums / jnp.maximum(list_counts, 1.0)[:, None]
    return (whitened, centroid_means)
```

```python
import functools

import jax
import jax.numpy as jnp
from jax import lax
from jax.experimental import pallas as pl
from jax.experimental.pallas import tpu as pltpu
from jax.sharding import PartitionSpec as P

CENTROIDS = 16384
BLOCK = 128
PANEL = 8


def split3(value):
    high = value.astype(jnp.bfloat16).astype(jnp.float32)
    rest = value - high
    mid = rest.astype(jnp.bfloat16).astype(jnp.float32)
    return high, mid, rest - mid


def dot(a, b, dims):
    return lax.dot_general(
        a, b, (dims, ((), ())), precision=lax.Precision.HIGHEST, preferred_element_type=jnp.float32
    )


def invert_block(d_ref, v_ref):
    def step(p, carry):
        row = pl.multiple_of(p * PANEL, PANEL)
        rows = d_ref[pl.ds(row, PANEL), :]
        left, right = rows[:, :BLOCK], rows[:, BLOCK:]
        rolled = pltpu.roll(left, lax.rem(BLOCK - row, BLOCK), 1)
        full = (PANEL, BLOCK)
        a = {}
        for j in range(PANEL):
            column = jnp.broadcast_to(rolled[:, j : j + 1], full)
            for i in range(j, PANEL):
                a[i, j] = jnp.broadcast_to(column[i : i + 1, :], full)
        u = [jnp.broadcast_to(left[i : i + 1, :], full) for i in range(PANEL)]
        v = [jnp.broadcast_to(right[i : i + 1, :], full) for i in range(PANEL)]
        for j in range(PANEL):
            scale = lax.rsqrt(a[j, j])
            u[j] = u[j] * scale
            v[j] = v[j] * scale
            for i in range(j + 1, PANEL):
                a[i, j] = a[i, j] * scale
            for i in range(j + 1, PANEL):
                for k in range(j + 1, i + 1):
                    a[i, k] = a[i, k] - a[i, j] * a[k, j]
                u[i] = u[i] - a[i, j] * u[j]
                v[i] = v[i] - a[i, j] * v[j]
        sub = lax.broadcasted_iota(jnp.int32, full, 0)
        up, vp = u[0], v[0]
        for i in range(1, PANEL):
            up = jnp.where(sub == i, u[i], up)
            vp = jnp.where(sub == i, v[i], vp)
        v_ref[pl.ds(row, PANEL), :] = vp
        uh, um, ul = split3(up)
        vh, vm, vl = split3(vp)
        lhs = jnp.concatenate([uh, uh, um, uh, um, ul], axis=0).astype(jnp.bfloat16)
        rhs = jnp.concatenate(
            [
                jnp.concatenate([uh, um, uh, ul, um, uh], axis=0),
                jnp.concatenate([vh, vm, vh, vl, vm, vh], axis=0),
            ],
            axis=1,
        ).astype(jnp.bfloat16)
        d_ref[...] = d_ref[...] - lax.dot_general(
            lhs, rhs, (((0,), (0,)), ((), ())), preferred_element_type=jnp.float32
        )
        return carry

    lax.fori_loop(0, BLOCK // PANEL, step, 0)


def factor_kernel(total, gram_ref, e_ref, s_ref, n_ref, w_ref, m_ref, a_ref, x_ref, d_ref, v_ref):
    width = gram_ref.shape[0]
    r = lax.broadcasted_iota(jnp.int32, (BLOCK, BLOCK), 0)
    c = lax.broadcasted_iota(jnp.int32, (BLOCK, BLOCK), 1)
    eye = jnp.where(r == c, 1.0, 0.0).astype(jnp.float32)
    a_ref[...] = gram_ref[...] / total
    x_ref[...] = jnp.zeros_like(x_ref)
    for lo in range(0, width, BLOCK):
        hi = lo + BLOCK
        here = slice(lo, hi)
        d_ref[:, :BLOCK] = a_ref[here, here] + 1e-05 * eye
        d_ref[:, BLOCK:] = eye
        invert_block(d_ref, v_ref)
        inv = v_ref[...]
        x_ref[here, here] = inv
        if lo > 0:
            x_ref[here, :lo] = dot(inv, x_ref[here, :lo], ((1,), (0,)))
        if hi < width:
            upper = dot(inv, a_ref[here, hi:], ((1,), (0,)))
            a_ref[hi:, hi:] = a_ref[hi:, hi:] - dot(upper, upper, ((0,), (0,)))
            x_ref[hi:, :hi] = x_ref[hi:, :hi] - dot(upper, x_ref[here, :hi], ((0,), (0,)))
    w_ref[...] = dot(e_ref[...], x_ref[...], ((1,), (1,)))
    m_ref[...] = dot(s_ref[...], x_ref[...], ((1,), (1,))) / jnp.maximum(n_ref[...], 1.0)


def factor_and_solve(gram, embeddings, sums, counts, total):
    width = gram.shape[0]
    vmem = pl.BlockSpec(memory_space=pltpu.VMEM)
    return pl.pallas_call(
        functools.partial(factor_kernel, float(total)),
        out_shape=(
            jax.ShapeDtypeStruct(embeddings.shape, jnp.float32),
            jax.ShapeDtypeStruct(sums.shape, jnp.float32),
        ),
        in_specs=[vmem] * 4,
        out_specs=(vmem, vmem),
        scratch_shapes=[
            pltpu.VMEM((width, width), jnp.float32),
            pltpu.VMEM((width, width), jnp.float32),
            pltpu.VMEM((BLOCK, 2 * BLOCK), jnp.float32),
            pltpu.VMEM((BLOCK, BLOCK), jnp.float32),
        ],
        compiler_params=pltpu.CompilerParams(vmem_limit_bytes=48 * 1024 * 1024),
    )(gram, embeddings, sums, counts)


def body(embeddings, assignments):
    rows_here = embeddings.shape[0]
    width = embeddings.shape[1]
    owners = lax.axis_size("rows")
    groups = lax.axis_size("grp")
    total = rows_here * owners * groups
    partial_value = jnp.dot(
        embeddings.T,
        embeddings,
        precision=lax.Precision.HIGHEST,
        preferred_element_type=jnp.float32,
    )
    gram = lax.psum(partial_value, ("rows", "grp"))
    per_owner = CENTROIDS // owners
    capacity = max(2, 2 * rows_here // owners)
    target = assignments // per_owner
    local = assignments % per_owner
    hits = (target[:, None] == jnp.arange(owners, dtype=jnp.int32)[None, :]).astype(jnp.int32)
    rank = jnp.sum(hits * (jnp.cumsum(hits, axis=0) - 1), axis=1)
    slot = target * capacity + rank
    outgoing = jnp.zeros((owners * capacity, width), jnp.float32).at[slot].set(embeddings)
    labels = jnp.full((owners * capacity,), -1, jnp.int32).at[slot].set(local)
    incoming, tags = (
        lax.all_to_all(
            outgoing.reshape(owners, capacity, width),
            "rows",
            split_axis=0,
            concat_axis=0,
            tiled=True,
        ),
        lax.all_to_all(
            labels.reshape(owners, capacity), "rows", split_axis=0, concat_axis=0, tiled=True
        ),
    )
    member = (tags.reshape(-1)[None, :] == jnp.arange(per_owner, dtype=jnp.int32)[:, None]).astype(
        jnp.float32
    )
    list_sums = jnp.dot(
        member,
        incoming.reshape(-1, width),
        precision=lax.Precision.HIGHEST,
        preferred_element_type=jnp.float32,
    )
    list_counts = jnp.sum(member, axis=1)
    list_sums, list_counts = (
        lax.psum_scatter(list_sums, "grp", scatter_dimension=0, tiled=True),
        lax.psum_scatter(list_counts, "grp", scatter_dimension=0, tiled=True),
    )
    return factor_and_solve(gram, embeddings, list_sums, list_counts[:, None], total)


def solution(mesh):
    return jax.shard_map(
        body,
        mesh=mesh,
        in_specs=(P(("rows", "grp"), None), P(("rows", "grp"))),
        out_specs=(P(("rows", "grp"), None), P(("rows", "grp"), None)),
        check_vma=False,
    )
```

```python
import functools

import jax
import jax.numpy as jnp
from jax import lax
from jax.experimental import pallas as pl
from jax.experimental.pallas import tpu as pltpu
from jax.sharding import PartitionSpec as P

CENTROIDS = 16384
BLOCK = 128
PANEL = 8


def split3(value):
    high = value.astype(jnp.bfloat16).astype(jnp.float32)
    rest = value - high
    mid = rest.astype(jnp.bfloat16).astype(jnp.float32)
    return high, mid, rest - mid


def dot(a, b, dims):
    return lax.dot_general(
        a, b, (dims, ((), ())), precision=lax.Precision.HIGHEST, preferred_element_type=jnp.float32
    )


def invert_block(d_ref, v_ref):
    def step(p, carry):
        row = pl.multiple_of(p * PANEL, PANEL)
        rows = d_ref[pl.ds(row, PANEL), :]
        left, right = rows[:, :BLOCK], rows[:, BLOCK:]
        rolled = pltpu.roll(left, lax.rem(BLOCK - row, BLOCK), 1)
        full = (PANEL, BLOCK)
        a = {}
        for j in range(PANEL):
            column = jnp.broadcast_to(rolled[:, j : j + 1], full)
            for i in range(j, PANEL):
                a[i, j] = jnp.broadcast_to(column[i : i + 1, :], full)
        u = [jnp.broadcast_to(left[i : i + 1, :], full) for i in range(PANEL)]
        v = [jnp.broadcast_to(right[i : i + 1, :], full) for i in range(PANEL)]
        for j in range(PANEL):
            scale = lax.rsqrt(a[j, j])
            u[j] = u[j] * scale
            v[j] = v[j] * scale
            for i in range(j + 1, PANEL):
                a[i, j] = a[i, j] * scale
            for i in range(j + 1, PANEL):
                for k in range(j + 1, i + 1):
                    a[i, k] = a[i, k] - a[i, j] * a[k, j]
                u[i] = u[i] - a[i, j] * u[j]
                v[i] = v[i] - a[i, j] * v[j]
        sub = lax.broadcasted_iota(jnp.int32, full, 0)
        up, vp = u[0], v[0]
        for i in range(1, PANEL):
            up = jnp.where(sub == i, u[i], up)
            vp = jnp.where(sub == i, v[i], vp)
        v_ref[pl.ds(row, PANEL), :] = vp
        uh, um, ul = split3(up)
        vh, vm, vl = split3(vp)
        lhs = jnp.concatenate([uh, uh, um, uh, um, ul], axis=0).astype(jnp.bfloat16)
        rhs = jnp.concatenate(
            [
                jnp.concatenate([uh, um, uh, ul, um, uh], axis=0),
                jnp.concatenate([vh, vm, vh, vl, vm, vh], axis=0),
            ],
            axis=1,
        ).astype(jnp.bfloat16)
        d_ref[...] = d_ref[...] - lax.dot_general(
            lhs, rhs, (((0,), (0,)), ((), ())), preferred_element_type=jnp.float32
        )
        return carry

    lax.fori_loop(0, BLOCK // PANEL, step, 0)


def block_pairs(width):
    blocks = width // BLOCK
    return [(i, j) for i in range(blocks) for j in range(i, blocks)]


def gram_kernel(e_ref, g_ref):
    width = e_ref.shape[1]
    used = 0
    for i in range(width // BLOCK):
        lo = i * BLOCK
        strip = dot(e_ref[:, lo : lo + BLOCK], e_ref[:, lo:], ((0,), (0,)))
        for j in range(strip.shape[1] // BLOCK):
            g_ref[used : used + BLOCK, :] = strip[:, j * BLOCK : (j + 1) * BLOCK]
            used += BLOCK
    if used < g_ref.shape[0]:
        g_ref[used:, :] = jnp.zeros((g_ref.shape[0] - used, BLOCK), jnp.float32)


def local_gram(embeddings, devices):
    width = embeddings.shape[1]
    unit = devices * 8
    rows = len(block_pairs(width)) * BLOCK
    rows = (rows + unit - 1) // unit * unit
    vmem = pl.BlockSpec(memory_space=pltpu.VMEM)
    return pl.pallas_call(
        gram_kernel,
        out_shape=jax.ShapeDtypeStruct((rows, BLOCK), jnp.float32),
        in_specs=[vmem],
        out_specs=vmem,
        compiler_params=pltpu.CompilerParams(vmem_limit_bytes=32 * 1024 * 1024),
    )(embeddings)


def reduce_kernel(links, g_ref, out_ref, acc_ref, in_ref, send_sem, recv_sem):
    partners, bits = [], []
    for axis, bit in links:
        me = lax.axis_index(axis)
        one = lax.rem(me // bit, 2)
        bits.append(one)
        partners.append({axis: me + bit - 2 * bit * one})
    barrier = pltpu.get_barrier_semaphore()
    for partner in partners:
        pl.semaphore_signal(
            barrier, inc=1, device_id=partner, device_id_type=pl.DeviceIdType.MESH
        )
    pl.semaphore_wait(barrier, len(partners))
    steps = len(links)
    size = g_ref.shape[0]
    start = 0
    starts = []
    landed = 0
    for k in range(steps):
        half = size // 2
        source = g_ref if k == 0 else acc_ref
        keep = pl.multiple_of(start + bits[k] * half, 8)
        give = pl.multiple_of(start + (1 - bits[k]) * half, 8)
        copy = pltpu.make_async_remote_copy(
            src_ref=source.at[pl.ds(give, half)],
            dst_ref=in_ref.at[pl.ds(landed, half)],
            send_sem=send_sem.at[k],
            recv_sem=recv_sem.at[k],
            device_id=partners[k],
            device_id_type=pl.DeviceIdType.MESH,
        )
        copy.start()
        copy.wait()
        total = source[pl.ds(keep, half), :] + in_ref[pl.ds(landed, half), :]
        if k == steps - 1:
            out_ref[pl.ds(keep, half), :] = total
        else:
            acc_ref[pl.ds(keep, half), :] = total
        landed += half
        start, size = keep, half
        starts.append(keep)
    for k in reversed(range(steps)):
        here = pl.ds(starts[k], size)
        copy = pltpu.make_async_remote_copy(
            src_ref=out_ref.at[here],
            dst_ref=out_ref.at[here],
            send_sem=send_sem.at[steps + k],
            recv_sem=recv_sem.at[steps + k],
            device_id=partners[k],
            device_id_type=pl.DeviceIdType.MESH,
        )
        copy.start()
        copy.wait()
        size *= 2


def reduce_everywhere(packed):
    links = []
    for axis in ("grp", "rows"):
        bit = 1
        while bit < lax.axis_size(axis):
            links.append((axis, bit))
            bit *= 2
    vmem = pl.BlockSpec(memory_space=pltpu.VMEM)
    return pl.pallas_call(
        functools.partial(reduce_kernel, links),
        out_shape=jax.ShapeDtypeStruct(packed.shape, jnp.float32),
        in_specs=[vmem],
        out_specs=vmem,
        scratch_shapes=[
            pltpu.VMEM(packed.shape, jnp.float32),
            pltpu.VMEM(packed.shape, jnp.float32),
            pltpu.SemaphoreType.DMA((2 * len(links),)),
            pltpu.SemaphoreType.DMA((2 * len(links),)),
        ],
        compiler_params=pltpu.CompilerParams(
            collective_id=0, has_side_effects=True, vmem_limit_bytes=24 * 1024 * 1024
        ),
    )(packed)


def factor_kernel(total, g_ref, e_ref, w_ref, x_ref, a_ref, d_ref, v_ref):
    width = x_ref.shape[0]
    r = lax.broadcasted_iota(jnp.int32, (BLOCK, BLOCK), 0)
    c = lax.broadcasted_iota(jnp.int32, (BLOCK, BLOCK), 1)
    eye = jnp.where(r == c, 1.0, 0.0).astype(jnp.float32)
    for n, (i, j) in enumerate(block_pairs(width)):
        a_ref[i * BLOCK : (i + 1) * BLOCK, j * BLOCK : (j + 1) * BLOCK] = (
            g_ref[n * BLOCK : (n + 1) * BLOCK, :] / total
        )
    x_ref[...] = jnp.zeros_like(x_ref)
    for lo in range(0, width, BLOCK):
        hi = lo + BLOCK
        here = slice(lo, hi)
        d_ref[:, :BLOCK] = a_ref[here, here] + 1e-05 * eye
        d_ref[:, BLOCK:] = eye
        invert_block(d_ref, v_ref)
        inv = v_ref[...]
        x_ref[here, here] = inv
        if lo > 0:
            x_ref[here, :lo] = dot(inv, x_ref[here, :lo], ((1,), (0,)))
        if hi < width:
            upper = dot(inv, a_ref[here, hi:], ((1,), (0,)))
            for row in range(hi, width, BLOCK):
                strip = slice(row, row + BLOCK)
                a_ref[strip, row:] = a_ref[strip, row:] - dot(
                    upper[:, row - hi : row - hi + BLOCK], upper[:, row - hi :], ((0,), (0,))
                )
            x_ref[hi:, :hi] = x_ref[hi:, :hi] - dot(upper, x_ref[here, :hi], ((0,), (0,)))
    w_ref[...] = dot(e_ref[...], x_ref[...], ((1,), (1,)))


def factor_and_whiten(packed, embeddings, total):
    width = embeddings.shape[1]
    vmem = pl.BlockSpec(memory_space=pltpu.VMEM)
    return pl.pallas_call(
        functools.partial(factor_kernel, float(total)),
        out_shape=(
            jax.ShapeDtypeStruct(embeddings.shape, jnp.float32),
            jax.ShapeDtypeStruct((width, width), jnp.float32),
        ),
        in_specs=[vmem] * 2,
        out_specs=(vmem, vmem),
        scratch_shapes=[
            pltpu.VMEM((width, width), jnp.float32),
            pltpu.VMEM((BLOCK, 2 * BLOCK), jnp.float32),
            pltpu.VMEM((BLOCK, BLOCK), jnp.float32),
        ],
        cost_estimate=pl.CostEstimate(
            flops=12 * width**3, bytes_accessed=12 * width**2, transcendentals=width
        ),
        compiler_params=pltpu.CompilerParams(vmem_limit_bytes=32 * 1024 * 1024),
    )(packed, embeddings)


def means_kernel(rows_ref, tags_ref, x_ref, m_ref):
    lists, width = m_ref.shape
    count = rows_ref.shape[0]
    index = lax.broadcasted_iota(jnp.int32, (lists, count), 0)
    base = lax.axis_index("grp") * lists
    hit = tags_ref[...].astype(jnp.int32) == index + (base + 1)
    member = jnp.where(hit, 1.0, 0.0).astype(jnp.float32)
    counts = jnp.sum(member, axis=1, keepdims=True)
    member = member.astype(jnp.bfloat16)
    sums = jnp.zeros((lists, width), jnp.float32)
    for part in split3(rows_ref[...]):
        sums = sums + lax.dot_general(
            member,
            part.astype(jnp.bfloat16),
            (((1,), (0,)), ((), ())),
            preferred_element_type=jnp.float32,
        )
    m_ref[...] = dot(sums, x_ref[...], ((1,), (1,))) / jnp.maximum(counts, 1.0)


def centroid_means_of(rows, tags, inverse, lists):
    width = inverse.shape[0]
    vmem = pl.BlockSpec(memory_space=pltpu.VMEM)
    return pl.pallas_call(
        means_kernel,
        out_shape=jax.ShapeDtypeStruct((lists, width), jnp.float32),
        in_specs=[vmem] * 3,
        out_specs=vmem,
        compiler_params=pltpu.CompilerParams(vmem_limit_bytes=48 * 1024 * 1024),
    )(rows, tags, inverse)


def body(embeddings, assignments):
    rows_here = embeddings.shape[0]
    width = embeddings.shape[1]
    owners = lax.axis_size("rows")
    groups = lax.axis_size("grp")
    total = rows_here * owners * groups
    gram = reduce_everywhere(local_gram(embeddings, owners * groups))
    whitened, inverse = factor_and_whiten(gram, embeddings, total)

    per_owner = CENTROIDS // owners
    capacity = max(2, 2 * rows_here // owners)
    target = assignments // per_owner
    local = assignments % per_owner
    hits = (target[:, None] == jnp.arange(owners, dtype=jnp.int32)[None, :]).astype(jnp.int32)
    rank = jnp.sum(hits * (jnp.cumsum(hits, axis=0) - 1), axis=1)
    slot = target * capacity + rank
    tagged = jnp.concatenate(
        [
            embeddings,
            jnp.broadcast_to((local + 1).astype(jnp.float32)[:, None], (rows_here, BLOCK)),
        ],
        axis=1,
    )
    outgoing = jnp.zeros((owners * capacity, width + BLOCK), jnp.float32).at[slot].set(tagged)
    incoming = lax.all_to_all(
        outgoing.reshape(owners, capacity, width + BLOCK),
        "rows",
        split_axis=0,
        concat_axis=0,
        tiled=True,
    )
    incoming = lax.all_gather(incoming.reshape(-1, width + BLOCK), "grp", axis=0, tiled=True)
    means = centroid_means_of(
        incoming[:, :width], incoming[:, width][None, :], inverse, per_owner // groups
    )
    return (whitened, means)


def solution(mesh):
    return jax.shard_map(
        body,
        mesh=mesh,
        in_specs=(P(("rows", "grp"), None), P(("rows", "grp"))),
        out_specs=(P(("rows", "grp"), None), P(("rows", "grp"), None)),
        check_vma=False,
    )
```

```python
import functools

import jax
import jax.numpy as jnp
from jax import lax
from jax.experimental import pallas as pl
from jax.experimental.pallas import tpu as pltpu
from jax.sharding import PartitionSpec as P

CENTROIDS = 16384
BLOCK = 128
PANEL = 8


def split3(value):
    high = value.astype(jnp.bfloat16).astype(jnp.float32)
    rest = value - high
    mid = rest.astype(jnp.bfloat16).astype(jnp.float32)
    return high, mid, rest - mid


def dot(a, b, dims):
    return lax.dot_general(
        a, b, (dims, ((), ())), precision=lax.Precision.HIGHEST, preferred_element_type=jnp.float32
    )


def solve_into(out_ref, values, x_ref, scale=None):
    width = x_ref.shape[0]
    strip = 2 * BLOCK if width % (2 * BLOCK) == 0 else BLOCK
    high, mid, _ = split3(values)
    high, mid = high.astype(jnp.bfloat16), mid.astype(jnp.bfloat16)
    for lo in range(0, width, strip):
        hi = lo + strip
        xh, xm, _ = split3(x_ref[lo:hi, :hi])
        xh, xm = xh.astype(jnp.bfloat16), xm.astype(jnp.bfloat16)
        out = jnp.zeros((values.shape[0], strip), jnp.float32)
        for a, b in ((mid, xh), (high, xm), (high, xh)):
            out = out + lax.dot_general(
                a[:, :hi], b, (((1,), (1,)), ((), ())), preferred_element_type=jnp.float32
            )
        if scale is None:
            out_ref[:, lo:hi] = out
        else:
            out_ref[:, lo:hi] = out * scale


def invert_block(d_ref, v_ref):
    def step(p, carry):
        row = pl.multiple_of(p * PANEL, PANEL)
        rows = d_ref[pl.ds(row, PANEL), :]
        left, right = rows[:, :BLOCK], rows[:, BLOCK:]
        rolled = pltpu.roll(left, lax.rem(BLOCK - row, BLOCK), 1)
        full = (PANEL, BLOCK)
        a = {}
        for j in range(PANEL):
            column = jnp.broadcast_to(rolled[:, j : j + 1], full)
            for i in range(j, PANEL):
                a[i, j] = jnp.broadcast_to(column[i : i + 1, :], full)
        u = [jnp.broadcast_to(left[i : i + 1, :], full) for i in range(PANEL)]
        v = [jnp.broadcast_to(right[i : i + 1, :], full) for i in range(PANEL)]
        for j in range(PANEL):
            scale = lax.rsqrt(a[j, j])
            u[j] = u[j] * scale
            v[j] = v[j] * scale
            for i in range(j + 1, PANEL):
                a[i, j] = a[i, j] * scale
            for i in range(j + 1, PANEL):
                for k in range(j + 1, i + 1):
                    a[i, k] = a[i, k] - a[i, j] * a[k, j]
                u[i] = u[i] - a[i, j] * u[j]
                v[i] = v[i] - a[i, j] * v[j]
        sub = lax.broadcasted_iota(jnp.int32, full, 0)
        up, vp = u[0], v[0]
        for i in range(1, PANEL):
            up = jnp.where(sub == i, u[i], up)
            vp = jnp.where(sub == i, v[i], vp)
        v_ref[pl.ds(row, PANEL), :] = vp
        uh, um, ul = split3(up)
        vh, vm, vl = split3(vp)
        lhs = jnp.concatenate([uh, uh, um, uh, um, ul], axis=0).astype(jnp.bfloat16)
        rhs = jnp.concatenate(
            [
                jnp.concatenate([uh, um, uh, ul, um, uh], axis=0),
                jnp.concatenate([vh, vm, vh, vl, vm, vh], axis=0),
            ],
            axis=1,
        ).astype(jnp.bfloat16)
        d_ref[...] = d_ref[...] - lax.dot_general(
            lhs, rhs, (((0,), (0,)), ((), ())), preferred_element_type=jnp.float32
        )
        return carry

    lax.fori_loop(0, BLOCK // PANEL, step, 0)


def block_pairs(width):
    blocks = width // BLOCK
    return [(i, j) for i in range(blocks) for j in range(i, blocks)]


def gram_kernel(e_ref, g_ref):
    width = e_ref.shape[1]
    used = 0
    for i in range(width // BLOCK):
        lo = i * BLOCK
        strip = dot(e_ref[:, lo : lo + BLOCK], e_ref[:, lo:], ((0,), (0,)))
        for j in range(strip.shape[1] // BLOCK):
            g_ref[used : used + BLOCK, :] = strip[:, j * BLOCK : (j + 1) * BLOCK]
            used += BLOCK
    if used < g_ref.shape[0]:
        g_ref[used:, :] = jnp.zeros((g_ref.shape[0] - used, BLOCK), jnp.float32)


def local_gram(embeddings, devices):
    width = embeddings.shape[1]
    unit = devices * 8
    rows = len(block_pairs(width)) * BLOCK
    rows = (rows + unit - 1) // unit * unit
    vmem = pl.BlockSpec(memory_space=pltpu.VMEM)
    return pl.pallas_call(
        gram_kernel,
        out_shape=jax.ShapeDtypeStruct((rows, BLOCK), jnp.float32),
        in_specs=[vmem],
        out_specs=vmem,
        compiler_params=pltpu.CompilerParams(vmem_limit_bytes=32 * 1024 * 1024),
    )(embeddings)


def reduce_kernel(links, g_ref, out_ref, acc_ref, in_ref, send_sem, recv_sem):
    partners, bits = [], []
    for axis, bit in links:
        me = lax.axis_index(axis)
        one = lax.rem(me // bit, 2)
        bits.append(one)
        partners.append({axis: me + bit - 2 * bit * one})
    barrier = pltpu.get_barrier_semaphore()
    for partner in partners:
        pl.semaphore_signal(
            barrier, inc=1, device_id=partner, device_id_type=pl.DeviceIdType.MESH
        )
    pl.semaphore_wait(barrier, len(partners))
    steps = len(links)
    unit = 8
    for axis in ("grp", "rows"):
        unit *= lax.axis_size(axis)
    units = g_ref.shape[0] // unit
    streams = max(1, min(3, units, steps - 1))
    orders, sizes, starts = [], [], []
    first = 0
    for n in range(streams):
        size = (units // streams + (1 if n < units % streams else 0)) * unit
        orders.append([0] + [1 + (n + k) % (steps - 1) for k in range(steps - 1)])
        sizes.append(size)
        starts.append([first])
        first += size
    landed = [s[0] for s in starts]

    def send(source, source_start, target, target_start, rows, link, slot):
        copy = pltpu.make_async_remote_copy(
            src_ref=source.at[pl.ds(source_start, rows)],
            dst_ref=target.at[pl.ds(target_start, rows)],
            send_sem=send_sem.at[slot],
            recv_sem=recv_sem.at[slot],
            device_id=partners[link],
            device_id_type=pl.DeviceIdType.MESH,
        )
        copy.start()
        return copy

    for k in range(steps):
        source = g_ref if k == 0 else acc_ref
        target = out_ref if k == steps - 1 else acc_ref
        copies = []
        for n in range(streams):
            link, start, half = orders[n][k], starts[n][-1], sizes[n] // 2
            keep = pl.multiple_of(start + bits[link] * half, 8)
            give = pl.multiple_of(start + (1 - bits[link]) * half, 8)
            slot = k * streams + n
            copies.append(send(source, give, in_ref, landed[n], half, link, slot))
            starts[n].append(keep)
        for n in range(streams):
            half, keep = sizes[n] // 2, starts[n][-1]
            copies[n].wait()
            target[pl.ds(keep, half), :] = (
                source[pl.ds(keep, half), :] + in_ref[pl.ds(landed[n], half), :]
            )
            landed[n] += half
            sizes[n] = half
    for k in reversed(range(steps)):
        copies = []
        for n in range(streams):
            start = starts[n][k + 1]
            slot = (steps + k) * streams + n
            copies.append(send(out_ref, start, out_ref, start, sizes[n], orders[n][k], slot))
        for n in range(streams):
            copies[n].wait()
            sizes[n] *= 2


def reduce_everywhere(packed):
    links = []
    for axis in ("grp", "rows"):
        bit = 1
        while bit < lax.axis_size(axis):
            links.append((axis, bit))
            bit *= 2
    vmem = pl.BlockSpec(memory_space=pltpu.VMEM)
    return pl.pallas_call(
        functools.partial(reduce_kernel, links),
        out_shape=jax.ShapeDtypeStruct(packed.shape, jnp.float32),
        in_specs=[vmem],
        out_specs=vmem,
        scratch_shapes=[
            pltpu.VMEM(packed.shape, jnp.float32),
            pltpu.VMEM(packed.shape, jnp.float32),
            pltpu.SemaphoreType.DMA((6 * len(links),)),
            pltpu.SemaphoreType.DMA((6 * len(links),)),
        ],
        compiler_params=pltpu.CompilerParams(
            collective_id=0, has_side_effects=True, vmem_limit_bytes=24 * 1024 * 1024
        ),
    )(packed)


def factor_kernel(total, g_ref, e_ref, w_ref, x_ref, a_ref, d_ref, v_ref):
    width = x_ref.shape[0]
    r = lax.broadcasted_iota(jnp.int32, (BLOCK, BLOCK), 0)
    c = lax.broadcasted_iota(jnp.int32, (BLOCK, BLOCK), 1)
    eye = jnp.where(r == c, 1.0, 0.0).astype(jnp.float32)
    for n, (i, j) in enumerate(block_pairs(width)):
        a_ref[i * BLOCK : (i + 1) * BLOCK, j * BLOCK : (j + 1) * BLOCK] = (
            g_ref[n * BLOCK : (n + 1) * BLOCK, :] / total
        )
    x_ref[...] = jnp.zeros_like(x_ref)
    for lo in range(0, width, BLOCK):
        hi = lo + BLOCK
        here = slice(lo, hi)
        d_ref[:, :BLOCK] = a_ref[here, here] + 1e-05 * eye
        d_ref[:, BLOCK:] = eye
        invert_block(d_ref, v_ref)
        inv = v_ref[...]
        x_ref[here, here] = inv
        if lo > 0:
            x_ref[here, :lo] = dot(inv, x_ref[here, :lo], ((1,), (0,)))
        if hi < width:
            upper = dot(inv, a_ref[here, hi:], ((1,), (0,)))
            for row in range(hi, width, BLOCK):
                strip = slice(row, row + BLOCK)
                a_ref[strip, row:] = a_ref[strip, row:] - dot(
                    upper[:, row - hi : row - hi + BLOCK], upper[:, row - hi :], ((0,), (0,))
                )
            x_ref[hi:, :hi] = x_ref[hi:, :hi] - dot(upper, x_ref[here, :hi], ((0,), (0,)))
    solve_into(w_ref, e_ref[...], x_ref)


def factor_and_whiten(packed, embeddings, total):
    width = embeddings.shape[1]
    vmem = pl.BlockSpec(memory_space=pltpu.VMEM)
    return pl.pallas_call(
        functools.partial(factor_kernel, float(total)),
        out_shape=(
            jax.ShapeDtypeStruct(embeddings.shape, jnp.float32),
            jax.ShapeDtypeStruct((width, width), jnp.float32),
        ),
        in_specs=[vmem] * 2,
        out_specs=(vmem, vmem),
        scratch_shapes=[
            pltpu.VMEM((width, width), jnp.float32),
            pltpu.VMEM((BLOCK, 2 * BLOCK), jnp.float32),
            pltpu.VMEM((BLOCK, BLOCK), jnp.float32),
        ],
        cost_estimate=pl.CostEstimate(
            flops=12 * width**3, bytes_accessed=12 * width**2, transcendentals=width
        ),
        compiler_params=pltpu.CompilerParams(vmem_limit_bytes=32 * 1024 * 1024),
    )(packed, embeddings)


def means_kernel(*refs):
    parts, x_ref, m_ref, s_ref, c_ref = refs[:-4], refs[-4], refs[-3], refs[-2], refs[-1]
    lists, width = m_ref.shape
    base = lax.axis_index("grp") * lists + 1
    for n, part in enumerate(parts):
        count = part.shape[0]
        tags = part[:, width:]
        lane = lax.broadcasted_iota(jnp.int32, (count, BLOCK), 1).astype(jnp.float32)
        members = []
        for lo in range(0, lists, BLOCK):
            members.append(jnp.where(tags == lane + (base + lo).astype(jnp.float32), 1.0, 0.0))
        if lists < BLOCK:
            members[0] = members[0][:, :lists]
        member = jnp.concatenate(members, axis=1).astype(jnp.bfloat16)
        dims = (((0,), (0,)), ((), ()))
        sums = jnp.zeros((lists, width), jnp.float32)
        for piece in split3(part[:, :width]):
            sums = sums + lax.dot_general(
                member, piece.astype(jnp.bfloat16), dims, preferred_element_type=jnp.float32
            )
        counts = lax.dot_general(
            member,
            jnp.ones((count, BLOCK), jnp.bfloat16),
            dims,
            preferred_element_type=jnp.float32,
        )
        if n == 0:
            s_ref[...] = sums
            c_ref[...] = counts
        else:
            s_ref[...] = s_ref[...] + sums
            c_ref[...] = c_ref[...] + counts
    solve_into(m_ref, s_ref[...], x_ref, 1.0 / jnp.maximum(c_ref[:, :1], 1.0))


def centroid_means_of(parts, inverse, lists):
    width = inverse.shape[0]
    vmem = pl.BlockSpec(memory_space=pltpu.VMEM)
    return pl.pallas_call(
        means_kernel,
        out_shape=jax.ShapeDtypeStruct((lists, width), jnp.float32),
        in_specs=[vmem] * (len(parts) + 1),
        out_specs=vmem,
        scratch_shapes=[
            pltpu.VMEM((lists, width), jnp.float32),
            pltpu.VMEM((lists, BLOCK), jnp.float32),
        ],
        compiler_params=pltpu.CompilerParams(vmem_limit_bytes=40 * 1024 * 1024),
    )(*parts, inverse)


def exchange(outgoing, owners):
    if owners > 16:
        got = lax.all_to_all(outgoing, "rows", split_axis=0, concat_axis=0, tiled=True)
        return got.reshape(-1, got.shape[-1])
    me = lax.axis_index("rows")
    got = [lax.dynamic_index_in_dim(outgoing, me, 0, keepdims=False)]
    for shift in range(1, owners):
        block = lax.dynamic_index_in_dim(outgoing, (me + shift) % owners, 0, keepdims=False)
        got.append(
            lax.ppermute(block, "rows", [(i, (i + shift) % owners) for i in range(owners)])
        )
    return jnp.concatenate(got, axis=0)


def body(embeddings, assignments):
    rows_here = embeddings.shape[0]
    width = embeddings.shape[1]
    owners = lax.axis_size("rows")
    groups = lax.axis_size("grp")
    total = rows_here * owners * groups
    gram = reduce_everywhere(local_gram(embeddings, owners * groups))
    whitened, inverse = factor_and_whiten(gram, embeddings, total)

    per_owner = CENTROIDS // owners
    capacity = max(2, 2 * rows_here // owners)
    target = assignments // per_owner
    local = assignments % per_owner
    hits = (target[:, None] == jnp.arange(owners, dtype=jnp.int32)[None, :]).astype(jnp.int32)
    rank = jnp.sum(hits * (jnp.cumsum(hits, axis=0) - 1), axis=1)
    slot = target * capacity + rank
    tagged = jnp.concatenate(
        [
            embeddings,
            jnp.broadcast_to((local + 1).astype(jnp.float32)[:, None], (rows_here, BLOCK)),
        ],
        axis=1,
    )
    outgoing = jnp.zeros((owners * capacity, width + BLOCK), jnp.float32).at[slot].set(tagged)
    incoming = exchange(outgoing.reshape(owners, capacity, width + BLOCK), owners)
    parts = [incoming]
    for shift in range(1, groups):
        parts.append(
            lax.ppermute(incoming, "grp", [(i, (i + shift) % groups) for i in range(groups)])
        )
    means = centroid_means_of(parts, inverse, per_owner // groups)
    return (whitened, means)


def solution(mesh):
    return jax.shard_map(
        body,
        mesh=mesh,
        in_specs=(P(("rows", "grp"), None), P(("rows", "grp"))),
        out_specs=(P(("rows", "grp"), None), P(("rows", "grp"), None)),
        check_vma=False,
    )
```

```python
import functools

import jax
import jax.numpy as jnp
from jax import lax
from jax.experimental import pallas as pl
from jax.experimental.pallas import tpu as pltpu
from jax.sharding import PartitionSpec as P

CENTROIDS = 16384
BLOCK = 128
PANEL = 8


def split3(value):
    high = value.astype(jnp.bfloat16).astype(jnp.float32)
    rest = value - high
    mid = rest.astype(jnp.bfloat16).astype(jnp.float32)
    return high, mid, rest - mid


def dot(a, b, dims):
    return lax.dot_general(
        a, b, (dims, ((), ())), precision=lax.Precision.HIGHEST, preferred_element_type=jnp.float32
    )


def solve_into(out_ref, values, x_ref, scale=None):
    width = x_ref.shape[0]
    strip = 2 * BLOCK if width % (2 * BLOCK) == 0 else BLOCK
    high, mid, _ = split3(values)
    high, mid = high.astype(jnp.bfloat16), mid.astype(jnp.bfloat16)
    for lo in range(0, width, strip):
        hi = lo + strip
        xh, xm, _ = split3(x_ref[lo:hi, :hi])
        xh, xm = xh.astype(jnp.bfloat16), xm.astype(jnp.bfloat16)
        out = jnp.zeros((values.shape[0], strip), jnp.float32)
        for a, b in ((mid, xh), (high, xm), (high, xh)):
            out = out + lax.dot_general(
                a[:, :hi], b, (((1,), (1,)), ((), ())), preferred_element_type=jnp.float32
            )
        if scale is None:
            out_ref[:, lo:hi] = out
        else:
            out_ref[:, lo:hi] = out * scale


def invert_block(d_ref, v_ref):
    def step(p, carry):
        row = pl.multiple_of(p * PANEL, PANEL)
        rows = d_ref[pl.ds(row, PANEL), :]
        left, right = rows[:, :BLOCK], rows[:, BLOCK:]
        rolled = pltpu.roll(left, lax.rem(BLOCK - row, BLOCK), 1)
        full = (PANEL, BLOCK)
        a = {}
        for j in range(PANEL):
            column = jnp.broadcast_to(rolled[:, j : j + 1], full)
            for i in range(j, PANEL):
                a[i, j] = jnp.broadcast_to(column[i : i + 1, :], full)
        u = [jnp.broadcast_to(left[i : i + 1, :], full) for i in range(PANEL)]
        v = [jnp.broadcast_to(right[i : i + 1, :], full) for i in range(PANEL)]
        for j in range(PANEL):
            scale = lax.rsqrt(a[j, j])
            u[j] = u[j] * scale
            v[j] = v[j] * scale
            for i in range(j + 1, PANEL):
                a[i, j] = a[i, j] * scale
            for i in range(j + 1, PANEL):
                for k in range(j + 1, i + 1):
                    a[i, k] = a[i, k] - a[i, j] * a[k, j]
                u[i] = u[i] - a[i, j] * u[j]
                v[i] = v[i] - a[i, j] * v[j]
        sub = lax.broadcasted_iota(jnp.int32, full, 0)
        up, vp = u[0], v[0]
        for i in range(1, PANEL):
            up = jnp.where(sub == i, u[i], up)
            vp = jnp.where(sub == i, v[i], vp)
        v_ref[pl.ds(row, PANEL), :] = vp
        uh, um, ul = split3(up)
        vh, vm, vl = split3(vp)
        lhs = jnp.concatenate([uh, uh, um, uh, um, ul], axis=0).astype(jnp.bfloat16)
        rhs = jnp.concatenate(
            [
                jnp.concatenate([uh, um, uh, ul, um, uh], axis=0),
                jnp.concatenate([vh, vm, vh, vl, vm, vh], axis=0),
            ],
            axis=1,
        ).astype(jnp.bfloat16)
        d_ref[...] = d_ref[...] - lax.dot_general(
            lhs, rhs, (((0,), (0,)), ((), ())), preferred_element_type=jnp.float32
        )
        return carry

    lax.fori_loop(0, BLOCK // PANEL, step, 0)


def block_pairs(width):
    blocks = width // BLOCK
    return [(i, j) for i in range(blocks) for j in range(i, blocks)]


def gram_kernel(e_ref, g_ref):
    width = e_ref.shape[1]
    used = 0
    for i in range(width // BLOCK):
        lo = i * BLOCK
        strip = dot(e_ref[:, lo : lo + BLOCK], e_ref[:, lo:], ((0,), (0,)))
        for j in range(strip.shape[1] // BLOCK):
            g_ref[used : used + BLOCK, :] = strip[:, j * BLOCK : (j + 1) * BLOCK]
            used += BLOCK
    if used < g_ref.shape[0]:
        g_ref[used:, :] = jnp.zeros((g_ref.shape[0] - used, BLOCK), jnp.float32)


def local_gram(embeddings, devices):
    width = embeddings.shape[1]
    unit = devices * 8
    rows = len(block_pairs(width)) * BLOCK
    rows = (rows + unit - 1) // unit * unit
    vmem = pl.BlockSpec(memory_space=pltpu.VMEM)
    return pl.pallas_call(
        gram_kernel,
        out_shape=jax.ShapeDtypeStruct((rows, BLOCK), jnp.float32),
        in_specs=[vmem],
        out_specs=vmem,
        compiler_params=pltpu.CompilerParams(vmem_limit_bytes=32 * 1024 * 1024),
    )(embeddings)


def reduce_kernel(links, g_ref, out_ref, acc_ref, in_ref, send_sem, recv_sem):
    partners, bits = [], []
    for axis, bit in links:
        me = lax.axis_index(axis)
        one = lax.rem(me // bit, 2)
        bits.append(one)
        partners.append({axis: me + bit - 2 * bit * one})
    barrier = pltpu.get_barrier_semaphore()
    for partner in partners:
        pl.semaphore_signal(
            barrier, inc=1, device_id=partner, device_id_type=pl.DeviceIdType.MESH
        )
    pl.semaphore_wait(barrier, len(partners))
    steps = len(links)
    unit = 8
    for axis in ("grp", "rows"):
        unit *= lax.axis_size(axis)
    units = g_ref.shape[0] // unit
    streams = max(1, min(3, units, steps - 1))
    orders, sizes, starts = [], [], []
    first = 0
    for n in range(streams):
        size = (units // streams + (1 if n < units % streams else 0)) * unit
        orders.append([0] + [1 + (n + k) % (steps - 1) for k in range(steps - 1)])
        sizes.append(size)
        starts.append([first])
        first += size
    landed = [s[0] for s in starts]

    def send(source, source_start, target, target_start, rows, link, slot):
        copy = pltpu.make_async_remote_copy(
            src_ref=source.at[pl.ds(source_start, rows)],
            dst_ref=target.at[pl.ds(target_start, rows)],
            send_sem=send_sem.at[slot],
            recv_sem=recv_sem.at[slot],
            device_id=partners[link],
            device_id_type=pl.DeviceIdType.MESH,
        )
        copy.start()
        return copy

    for k in range(steps):
        source = g_ref if k == 0 else acc_ref
        target = out_ref if k == steps - 1 else acc_ref
        copies = []
        for n in range(streams):
            link, start, half = orders[n][k], starts[n][-1], sizes[n] // 2
            keep = pl.multiple_of(start + bits[link] * half, 8)
            give = pl.multiple_of(start + (1 - bits[link]) * half, 8)
            slot = k * streams + n
            copies.append(send(source, give, in_ref, landed[n], half, link, slot))
            starts[n].append(keep)
        for n in range(streams):
            half, keep = sizes[n] // 2, starts[n][-1]
            copies[n].wait()
            target[pl.ds(keep, half), :] = (
                source[pl.ds(keep, half), :] + in_ref[pl.ds(landed[n], half), :]
            )
            landed[n] += half
            sizes[n] = half
    for k in reversed(range(steps)):
        copies = []
        for n in range(streams):
            start = starts[n][k + 1]
            slot = (steps + k) * streams + n
            copies.append(send(out_ref, start, out_ref, start, sizes[n], orders[n][k], slot))
        for n in range(streams):
            copies[n].wait()
            sizes[n] *= 2


def reduce_everywhere(packed):
    links = []
    for axis in ("grp", "rows"):
        bit = 1
        while bit < lax.axis_size(axis):
            links.append((axis, bit))
            bit *= 2
    vmem = pl.BlockSpec(memory_space=pltpu.VMEM)
    return pl.pallas_call(
        functools.partial(reduce_kernel, links),
        out_shape=jax.ShapeDtypeStruct(packed.shape, jnp.float32),
        in_specs=[vmem],
        out_specs=vmem,
        scratch_shapes=[
            pltpu.VMEM(packed.shape, jnp.float32),
            pltpu.VMEM(packed.shape, jnp.float32),
            pltpu.SemaphoreType.DMA((6 * len(links),)),
            pltpu.SemaphoreType.DMA((6 * len(links),)),
        ],
        compiler_params=pltpu.CompilerParams(
            collective_id=0, has_side_effects=True, vmem_limit_bytes=24 * 1024 * 1024
        ),
    )(packed)


def factor_kernel(total, g_ref, e_ref, w_ref, x_ref, a_ref, d_ref, v_ref):
    width = x_ref.shape[0]
    r = lax.broadcasted_iota(jnp.int32, (BLOCK, BLOCK), 0)
    c = lax.broadcasted_iota(jnp.int32, (BLOCK, BLOCK), 1)
    eye = jnp.where(r == c, 1.0, 0.0).astype(jnp.float32)
    for n, (i, j) in enumerate(block_pairs(width)):
        a_ref[i * BLOCK : (i + 1) * BLOCK, j * BLOCK : (j + 1) * BLOCK] = (
            g_ref[n * BLOCK : (n + 1) * BLOCK, :] / total
        )
    x_ref[...] = jnp.zeros_like(x_ref)
    for lo in range(0, width, BLOCK):
        hi = lo + BLOCK
        here = slice(lo, hi)
        d_ref[:, :BLOCK] = a_ref[here, here] + 1e-05 * eye
        d_ref[:, BLOCK:] = eye
        invert_block(d_ref, v_ref)
        inv = v_ref[...]
        x_ref[here, here] = inv
        if lo > 0:
            x_ref[here, :lo] = dot(inv, x_ref[here, :lo], ((1,), (0,)))
        if hi < width:
            upper = dot(inv, a_ref[here, hi:], ((1,), (0,)))
            for row in range(hi, width, BLOCK):
                strip = slice(row, row + BLOCK)
                a_ref[strip, row:] = a_ref[strip, row:] - dot(
                    upper[:, row - hi : row - hi + BLOCK], upper[:, row - hi :], ((0,), (0,))
                )
            x_ref[hi:, :hi] = x_ref[hi:, :hi] - dot(upper, x_ref[here, :hi], ((0,), (0,)))
    solve_into(w_ref, e_ref[...], x_ref)


def factor_and_whiten(packed, embeddings, total):
    width = embeddings.shape[1]
    vmem = pl.BlockSpec(memory_space=pltpu.VMEM)
    return pl.pallas_call(
        functools.partial(factor_kernel, float(total)),
        out_shape=(
            jax.ShapeDtypeStruct(embeddings.shape, jnp.float32),
            jax.ShapeDtypeStruct((width, width), jnp.float32),
        ),
        in_specs=[vmem] * 2,
        out_specs=(vmem, vmem),
        scratch_shapes=[
            pltpu.VMEM((width, width), jnp.float32),
            pltpu.VMEM((BLOCK, 2 * BLOCK), jnp.float32),
            pltpu.VMEM((BLOCK, BLOCK), jnp.float32),
        ],
        cost_estimate=pl.CostEstimate(
            flops=12 * width**3, bytes_accessed=12 * width**2, transcendentals=width
        ),
        compiler_params=pltpu.CompilerParams(vmem_limit_bytes=32 * 1024 * 1024),
    )(packed, embeddings)


def means_kernel(*refs):
    parts, x_ref, m_ref, s_ref, c_ref = refs[:-4], refs[-4], refs[-3], refs[-2], refs[-1]
    lists, width = m_ref.shape
    base = lax.axis_index("grp") * lists + 1
    for n, part in enumerate(parts):
        count = part.shape[0]
        tags = part[:, width:]
        lane = lax.broadcasted_iota(jnp.int32, (count, BLOCK), 1).astype(jnp.float32)
        members = []
        for lo in range(0, lists, BLOCK):
            members.append(jnp.where(tags == lane + (base + lo).astype(jnp.float32), 1.0, 0.0))
        if lists < BLOCK:
            members[0] = members[0][:, :lists]
        member = jnp.concatenate(members, axis=1).astype(jnp.bfloat16)
        dims = (((0,), (0,)), ((), ()))
        sums = jnp.zeros((lists, width), jnp.float32)
        for piece in split3(part[:, :width]):
            sums = sums + lax.dot_general(
                member, piece.astype(jnp.bfloat16), dims, preferred_element_type=jnp.float32
            )
        counts = lax.dot_general(
            member,
            jnp.ones((count, BLOCK), jnp.bfloat16),
            dims,
            preferred_element_type=jnp.float32,
        )
        if n == 0:
            s_ref[...] = sums
            c_ref[...] = counts
        else:
            s_ref[...] = s_ref[...] + sums
            c_ref[...] = c_ref[...] + counts
    solve_into(m_ref, s_ref[...], x_ref, 1.0 / jnp.maximum(c_ref[:, :1], 1.0))


def centroid_means_of(parts, inverse, lists):
    width = inverse.shape[0]
    vmem = pl.BlockSpec(memory_space=pltpu.VMEM)
    return pl.pallas_call(
        means_kernel,
        out_shape=jax.ShapeDtypeStruct((lists, width), jnp.float32),
        in_specs=[vmem] * (len(parts) + 1),
        out_specs=vmem,
        scratch_shapes=[
            pltpu.VMEM((lists, width), jnp.float32),
            pltpu.VMEM((lists, BLOCK), jnp.float32),
        ],
        compiler_params=pltpu.CompilerParams(vmem_limit_bytes=40 * 1024 * 1024),
    )(*parts, inverse)


def exchange(outgoing, owners):
    if owners > 16:
        got = lax.all_to_all(outgoing, "rows", split_axis=0, concat_axis=0, tiled=True)
        return got.reshape(-1, got.shape[-1])
    me = lax.axis_index("rows")
    got = [lax.dynamic_index_in_dim(outgoing, me, 0, keepdims=False)]
    for shift in range(1, owners):
        block = lax.dynamic_index_in_dim(outgoing, (me + shift) % owners, 0, keepdims=False)
        got.append(
            lax.ppermute(block, "rows", [(i, (i + shift) % owners) for i in range(owners)])
        )
    return jnp.concatenate(got, axis=0)


def body(embeddings, assignments):
    rows_here = embeddings.shape[0]
    width = embeddings.shape[1]
    owners = lax.axis_size("rows")
    groups = lax.axis_size("grp")
    total = rows_here * owners * groups
    gram = reduce_everywhere(local_gram(embeddings, owners * groups))

    per_owner = CENTROIDS // owners
    capacity = max(2, 2 * rows_here // owners)
    target = assignments // per_owner
    local = assignments % per_owner
    hits = (target[:, None] == jnp.arange(owners, dtype=jnp.int32)[None, :]).astype(jnp.int32)
    rank = jnp.sum(hits * (jnp.cumsum(hits, axis=0) - 1), axis=1)
    slot = target * capacity + rank
    tagged = jnp.concatenate(
        [
            embeddings,
            jnp.broadcast_to((local + 1).astype(jnp.float32)[:, None], (rows_here, BLOCK)),
        ],
        axis=1,
    )
    outgoing = jnp.zeros((owners * capacity, width + BLOCK), jnp.float32).at[slot].set(tagged)
    incoming = exchange(outgoing.reshape(owners, capacity, width + BLOCK), owners)
    incoming, gram = lax.optimization_barrier((incoming, gram))
    whitened, inverse = factor_and_whiten(gram, embeddings, total)
    parts = [incoming]
    for shift in range(1, groups):
        parts.append(
            lax.ppermute(incoming, "grp", [(i, (i + shift) % groups) for i in range(groups)])
        )
    means = centroid_means_of(parts, inverse, per_owner // groups)
    return (whitened, means)


def solution(mesh):
    return jax.shard_map(
        body,
        mesh=mesh,
        in_specs=(P(("rows", "grp"), None), P(("rows", "grp"))),
        out_specs=(P(("rows", "grp"), None), P(("rows", "grp"), None)),
        check_vma=False,
    )
```
